32 devices in a mesh: passage: 4 (over z), list: 8 (over y, x, core).
Axes of the slice: x: 2, y: 2, z: 4, core: 2. Of those that a mesh axis runs over, the one named last changes fastest.
Arguments:
- passages: bfloat16 [16384, 1024], P(('passage', 'list')), may hold values from -6 to 6
- list_ids: int32 [16384], P(('passage', 'list')), may hold values from 0 to 16383, as said below
- old_centroids: float32 [16384, 1024], P(('passage', 'list')), may hold values from -6 to 6
- rotation: float32 [1024, 1024], replicated, may hold values from -0.1875 to 0.1875
Outputs:
- rotated: bfloat16 [16384, 1024], P(('passage', 'list'))
- centroids: float32 [16384, 1024], P(('passage', 'list'))
The draws below stay inside these ranges and needn't reach their ends.
Inputs may be any that keep to these rules, and one draw needn't show every extreme that they name: `list_ids`: on each device the ids of its 512 passages never fall. The lists o * 512 to (o + 1) * 512 - 1 belong to owner o, the device of index o along passage+list. At most 32 passages of one device fall in one owner's lists, and in every draw some owners take exactly 32 from every device.
All inputs are finite; a program needn't handle non-finite values.
Results may differ from the reference program's by a relative error of at most 0.001.
Values may be sent and summed in bfloat16 or wider, within the bound.
No kernel may reach another device: no remote copies, remote signals or barrier semaphores. Data moves between devices by JAX's collectives and lax.ppermute only.
A program may use at most 64 MiB of HBM per device.

```python
import jax
import jax.numpy as jnp
from jax import lax

D = 1024
LIST_DEV = 512
PDEV = 512
LISTS = 16384
PASSAGES = 16384
CAPO = 32
N_PASSAGE = 4
N_LIST = 8
DEVICES = 32


def draw_list_ids(key, part):
    key_pair, key_hot, key_cold, key_local = jax.random.split(jax.random.fold_in(key, 11), 4)
    half = N_PASSAGE // 2
    pick = jax.random.randint(key_pair, (DEVICES, half, N_LIST), 0, CAPO + 1)
    paired = jnp.concatenate([pick, CAPO - pick], axis=1)
    hot = jax.random.randint(key_hot, (), 0, N_LIST)
    cold = (hot + 1 + jax.random.randint(key_cold, (DEVICES,), 0, N_LIST - 1)) % N_LIST
    column = jnp.arange(N_LIST, dtype=jnp.int32)[None, None, :]
    loads = jnp.where(column == hot, CAPO, jnp.where(column == cold[:, None, None], 0, paired))
    loads = loads.reshape(DEVICES, DEVICES).astype(jnp.int32)
    ends = jnp.cumsum(loads, axis=1)
    positions = jnp.arange(PDEV, dtype=jnp.int32)
    owner = jnp.sum((positions[None, :, None] >= ends[:, None, :]).astype(jnp.int32), axis=2)
    local = jax.random.randint(key_local, (DEVICES, PDEV), 0, LIST_DEV)
    return jnp.sort(owner * LIST_DEV + local, axis=1).reshape(-1).astype(jnp.int32)


def steps_of(stream_key, shape, shards, smallest, top_value):
    gain = 1.0
    for axis_at, parts in shards:
        steps = jax.random.uniform(jax.random.fold_in(jax.random.fold_in(stream_key, 6), axis_at), (parts,), jnp.float32, smallest / len(shards), top_value / len(shards))
        gain = gain * jnp.repeat(jnp.exp(steps), shape[axis_at] // parts).reshape((-1,) + (1,) * (len(shape) - 1 - axis_at))
    return gain


def centred(key, dims, spread, most, pieces=(), kind=jnp.bfloat16):
    drawn = jax.random.normal(key, dims, jnp.float32) * spread
    if len(pieces) > 0:
        drawn = steps_of(key, dims, pieces, -0.22, 0.18) * drawn
    return jnp.clip(drawn, min=-most, max=most).astype(kind)


def setup_inputs(seed: int = 0) -> dict:
    splits = jax.random.split(jax.random.key(seed), 5)
    return {
        "passages": centred(splits[0], (PASSAGES, D), 1.0, 6.0, ((0, 32),)),
        "list_ids": draw_list_ids(jax.random.fold_in(splits[4], 71), 0),
        "old_centroids": centred(splits[2], (LISTS, D), 1.0, 6.0, ((0, 32),), jnp.float32),
        "rotation": centred(splits[3], (D, D), D ** -0.5, 0.1875, (), jnp.float32),
    }


def reference(passages, list_ids, old_centroids, rotation):
    values = passages.astype(jnp.float32)
    sums = jax.ops.segment_sum(values, list_ids, num_segments=LISTS)
    tally = jax.ops.segment_sum(jnp.ones(list_ids.shape, jnp.float32), list_ids, num_segments=LISTS)
    centroids = (sums + old_centroids) / (tally[:, None] + 1.0)
    residual = values - jnp.take(centroids, list_ids, axis=0)
    rotated = jnp.dot(residual, rotation, preferred_element_type=jnp.float32, precision=lax.Precision.HIGHEST)
    return rotated.astype(jnp.bfloat16), centroids
```

```python
import functools

import jax
import jax.numpy as jnp
from jax import lax
from jax.experimental import pallas as pl
from jax.experimental.pallas import tpu as pltpu
from jax.sharding import PartitionSpec as P

AXES = ("passage", "list")
BF16 = jnp.bfloat16
F32 = jnp.float32


def dot(a, b):
    return jnp.dot(a, b, preferred_element_type=F32)


def split3(value):
    high = value.astype(BF16)
    rest = value - high.astype(F32)
    middle = rest.astype(BF16)
    low = (rest - middle.astype(F32)).astype(BF16)
    return high, middle, low


def refine(chunk, rows_ref, ids_row_ref, ids_col_ref, old_ref, high_ref, low_ref, turned_ref, centroid_ref, parts_ref):
    slots = rows_ref.shape[0]
    lists = old_ref.shape[0]
    member = lax.broadcasted_iota(jnp.int32, (lists, slots), 0) == ids_row_ref[...]
    weight = member.astype(F32)
    tally = jnp.sum(weight, axis=1, keepdims=True)
    sums = dot(weight.astype(BF16), rows_ref[...])
    centroids = (sums + old_ref[...]) / (tally + 1.0)
    centroid_ref[...] = centroids
    for k, part in enumerate(split3(centroids)):
        parts_ref[k] = part

    def turn(step, carry):
        rows = pl.ds(pl.multiple_of(step * chunk, chunk), chunk)
        pick = lax.broadcasted_iota(jnp.int32, (chunk, lists), 1) == ids_col_ref[rows, :]
        pick = pick.astype(F32).astype(BF16)
        near = dot(pick, parts_ref[0]) + dot(pick, parts_ref[1]) + dot(pick, parts_ref[2])
        residual = rows_ref[rows, :].astype(F32) - near
        top = residual.astype(BF16)
        rest = (residual - top.astype(F32)).astype(BF16)
        out = dot(top, high_ref[...]) + (dot(top, low_ref[...]) + dot(rest, high_ref[...]))
        turned_ref[rows, :] = out.astype(BF16)
        return carry

    lax.fori_loop(0, slots // chunk, turn, 0)


def refined(rows, ids, old_centroids, high, low):
    slots, width = rows.shape
    lists = old_centroids.shape[0]
    chunk = 256 if slots % 256 == 0 else slots
    vmem = pl.BlockSpec(memory_space=pltpu.VMEM)
    return pl.pallas_call(
        functools.partial(refine, chunk),
        out_shape=(jax.ShapeDtypeStruct((slots, width), BF16), jax.ShapeDtypeStruct((lists, width), F32)),
        in_specs=[vmem] * 6,
        out_specs=(vmem, vmem),
        scratch_shapes=[pltpu.VMEM((3, lists, width), BF16)],
        compiler_params=pltpu.CompilerParams(vmem_limit_bytes=48 * 1024 * 1024),
        name="refine",
    )(rows, ids[None, :], ids[:, None], old_centroids, high, low)


def shards(passages, list_ids, old_centroids, rotation):
    devices = lax.axis_size("passage") * lax.axis_size("list")
    rows, width = passages.shape
    list_dev = old_centroids.shape[0]
    capacity = 2 * rows // devices
    owner_range = jnp.arange(devices, dtype=jnp.int32)
    starts = jnp.sum((list_ids[None, :] < (owner_range * list_dev)[:, None]).astype(jnp.int32), axis=1)
    slot_range = jnp.arange(capacity, dtype=jnp.int32)
    target = (starts[:, None] + slot_range[None, :]).reshape(-1)
    slot_owner = jnp.repeat(owner_range, capacity)
    select = (target[:, None] == jnp.arange(rows, dtype=jnp.int32)[None, :]) & (
        slot_owner[:, None] == (list_ids // list_dev)[None, :]
    )
    outgoing = dot(select.astype(BF16), passages).astype(BF16).reshape(devices, capacity, width)
    got_rows = lax.all_to_all(outgoing, AXES, split_axis=0, concat_axis=0, tiled=True)
    local = jnp.sum(jnp.where(select, (list_ids % list_dev - list_dev)[None, :], 0), axis=1) + list_dev
    got_ids = lax.all_to_all(local.reshape(devices, capacity), AXES, split_axis=0, concat_axis=0, tiled=True)
    high = lax.reduce_precision(rotation, 8, 7)
    low = (rotation - high).astype(BF16)
    high = high.astype(BF16)
    turned, centroids = refined(
        got_rows.reshape(devices * capacity, width), got_ids.reshape(-1), old_centroids, high, low
    )
    returned = lax.all_to_all(
        turned.reshape(devices, capacity, width), AXES, split_axis=0, concat_axis=0, tiled=True
    )
    rotated = lax.dot_general(
        select.astype(BF16),
        returned.reshape(devices * capacity, width),
        (((0,), (0,)), ((), ())),
        preferred_element_type=F32,
    ).astype(BF16)
    return rotated, centroids


def solution(mesh):
    in_specs = (P(AXES, None), P(AXES), P(AXES, None), P())
    out_specs = (P(AXES, None), P(AXES, None))
    return jax.shard_map(shards, mesh=mesh, in_specs=in_specs, out_specs=out_specs, check_vma=False)
```

```python
import functools

import jax
import jax.numpy as jnp
from jax import lax
from jax.experimental import pallas as pl
from jax.experimental.pallas import tpu as pltpu
from jax.sharding import PartitionSpec as P


AXES = ("passage", "list")
BF16 = jnp.bfloat16
F32 = jnp.float32
I32 = jnp.int32
VMEM = pl.BlockSpec(memory_space=pltpu.VMEM)
SMEM = pl.BlockSpec(memory_space=pltpu.SMEM)
TILE = 16


def dot(a, b):
    return jnp.dot(a, b, preferred_element_type=F32)


def iota(shape, axis):
    return lax.broadcasted_iota(I32, shape, axis)


def hot(condition):
    return condition.astype(F32).astype(BF16)


def split3(value):
    high = value.astype(BF16)
    rest = value - high.astype(F32)
    middle = rest.astype(BF16)
    low = (rest - middle.astype(F32)).astype(BF16)
    return high, middle, low


LIMIT = 24
CENTRE = 48


def centred(rows, ids, parts_ref):
    pick = hot(iota((rows.shape[0], parts_ref.shape[1]), 1) == ids)
    near = dot(pick, parts_ref[0]) + dot(pick, parts_ref[1]) + dot(pick, parts_ref[2])
    residual = rows.astype(F32) - near
    top = residual.astype(BF16)
    return top, (residual - top.astype(F32)).astype(BF16)


def turned(top, rest, high_ref, low_ref):
    out = dot(top, high_ref[...]) + (dot(top, low_ref[...]) + dot(rest, high_ref[...]))
    return out.astype(BF16)


def means(row_ref, old_ref, centroid_ref, parts_ref, pieces):
    lists = old_ref.shape[0]
    ids = row_ref[...]
    weight = (iota((lists, ids.shape[1]), 0) == ids).astype(F32)
    tally = jnp.sum(weight, axis=1, keepdims=True)
    weight = weight.astype(BF16)
    sums = None
    for begin, rows in pieces:
        part = dot(weight[:, begin : begin + rows.shape[0]], rows)
        sums = part if sums is None else sums + part
    centroids = (sums + old_ref[...]) / (tally + 1.0)
    centroid_ref[...] = centroids
    for k, part in enumerate(split3(centroids)):
        parts_ref[k] = part


def refine(chunk, rows_ref, row_ref, col_ref, old_ref, high_ref, low_ref, turned_ref, centroid_ref, parts_ref):
    means(row_ref, old_ref, centroid_ref, parts_ref, [(0, rows_ref[...])])

    def body(step, carry):
        rows = pl.ds(pl.multiple_of(step * chunk, chunk), chunk)
        top, rest = centred(rows_ref[rows, :], col_ref[rows, :], parts_ref)
        turned_ref[rows, :] = turned(top, rest, high_ref, low_ref)
        return carry

    lax.fori_loop(0, rows_ref.shape[0] // chunk, body, 0)


def ranks(devices, lists, ids):
    owner = ids // lists
    order = iota((devices, ids.shape[1]), 0)
    mine = order == owner
    starts = jnp.sum((ids < order * lists).astype(F32), axis=1, keepdims=True)
    start = jnp.sum(jnp.where(mine, starts, 0.0), axis=0, keepdims=True).astype(I32)
    return owner, iota(ids.shape, 1) - start, mine


def pack_ids(devices, capacity, lists, ids_ref, local_ref):
    ids = ids_ref[...]
    _, rank, mine = ranks(devices, lists, ids)
    rank = hot(iota((capacity, ids.shape[1]), 0) == rank)
    code = ids % lists + 1
    step = 32
    total = None
    for piece, scale in ((code // step, step), (code % step, 1)):
        part = jnp.where(mine, piece.astype(F32), 0.0).astype(BF16)
        found = lax.dot_general(part, rank, (((1,), (1,)), ((), ())), preferred_element_type=F32) * scale
        total = found if total is None else total + found
    local_ref[...] = total.astype(I32) - 1


def pack_far(devices, capacity, lists, group, me_ref, ids_ref, passages_ref, slot_ref, *out_refs):
    half = devices // 2
    owner, rank, _ = ranks(devices, lists, ids_ref[...])
    relative = jnp.bitwise_xor(owner, me_ref[0])
    block = jnp.where(relative >= half, relative - half, half + jnp.bitwise_and(owner, half - 1))
    slot = block * capacity + rank
    slot_ref[...] = slot
    size = out_refs[0].shape[0]
    for g in range(len(out_refs) // group):
        begin, count = g * group * size, group * size
        select = hot(iota((count, slot.shape[1]), 0) + begin == slot)
        rows = dot(select, passages_ref[...]).astype(BF16)
        for k in range(group):
            out_refs[g * group + k][...] = rows[k * size : (k + 1) * size]


def pack_near(slot_ref, passages_ref, out_ref):
    size = out_ref.shape[0]
    select = hot(iota((size, slot_ref.shape[1]), 0) + size == slot_ref[...])
    out_ref[...] = dot(select, passages_ref[...]).astype(BF16)


def gather_far(capacity, direct_refs, swap_refs, rows_ref):
    for k, (direct, swap) in enumerate(zip(direct_refs, swap_refs)):
        at = 2 * k * capacity
        rows_ref[at : at + capacity] = direct[0:capacity]
        rows_ref[at + capacity : at + 2 * capacity] = swap[capacity : 2 * capacity]


def spread(rows, out_refs):
    size = out_refs[0].shape[0]
    for k, ref in enumerate(out_refs):
        ref[...] = rows[k * size : (k + 1) * size]


def centre(pairs, first, capacity, *refs):
    direct_refs, swap_refs, refs = refs[:pairs], refs[pairs : 2 * pairs], refs[2 * pairs :]
    near_ref, row_ref, col_ref, old_ref, high_ref, low_ref, centroid_ref, parts_ref, held_ref = refs[:9]
    out_refs = refs[9:]
    gather_far(capacity, direct_refs, swap_refs, held_ref)
    far = held_ref.shape[0]
    means(row_ref, old_ref, centroid_ref, parts_ref, [(0, held_ref[...]), (far, near_ref[...])])
    count = 2 * first * capacity
    top, rest = centred(held_ref[0:count], col_ref[0:count], parts_ref)
    spread(turned(top, rest, high_ref, low_ref), out_refs)


def turn_far(begin, held_ref, col_ref, parts_ref, high_ref, low_ref, *out_refs):
    count = sum(ref.shape[0] for ref in out_refs)
    top, rest = centred(held_ref[begin : begin + count], col_ref[begin : begin + count], parts_ref)
    spread(turned(top, rest, high_ref, low_ref), out_refs)


def turn_near(chunks, near_ref, col_ref, parts_ref, high_ref, low_ref, out_ref):
    begin = col_ref.shape[0] - near_ref.shape[0]
    size = near_ref.shape[0] // chunks
    for c in range(chunks):
        at = c * size
        top, rest = centred(near_ref[at : at + size], col_ref[begin + at : begin + at + size], parts_ref)
        out_ref[at : at + size] = turned(top, rest, high_ref, low_ref)


def unpack(pairs, capacity, *refs):
    direct_refs, swap_refs, refs = refs[:pairs], refs[pairs : 2 * pairs], refs[2 * pairs :]
    near_ref, slot_ref, out_ref, rows_ref = refs
    gather_far(capacity, direct_refs, swap_refs, rows_ref)
    far, size = rows_ref.shape[0], slot_ref.shape[0]
    pick = hot(iota((size, far), 1) == slot_ref[...])
    other = hot(iota((size, near_ref.shape[0]), 1) + far == slot_ref[...])
    out_ref[...] = (dot(pick, rows_ref[...]) + dot(other, near_ref[...])).astype(BF16)


def call(body, inputs, outputs, scratch=(), flops=0, limit=LIMIT):
    outs = [jax.ShapeDtypeStruct(shape, kind) for shape, kind in outputs]
    size = sum(a.size * a.dtype.itemsize for a in list(inputs) + outs)
    return pl.pallas_call(
        body,
        out_shape=outs,
        in_specs=[SMEM if a.shape == (1,) else VMEM for a in inputs],
        out_specs=[VMEM] * len(outs),
        scratch_shapes=[pltpu.VMEM(shape, kind) for shape, kind in scratch],
        compiler_params=pltpu.CompilerParams(vmem_limit_bytes=limit * 1024 * 1024),
        cost_estimate=pl.CostEstimate(flops=flops, bytes_accessed=size, transcendentals=0),
    )(*inputs)


def split_rotation(rotation):
    high = lax.reduce_precision(rotation, 8, 7)
    low = (rotation - high).astype(BF16)
    return high.astype(BF16), low


def whole_exchange(passages, list_ids, old_centroids, rotation, devices, capacity):
    rows, width = passages.shape
    lists = old_centroids.shape[0]
    slots = devices * capacity
    owners = jnp.arange(devices, dtype=I32)
    starts = jnp.sum((list_ids[None, :] < (owners * lists)[:, None]).astype(I32), axis=1)
    target = (starts[:, None] + jnp.arange(capacity, dtype=I32)[None, :]).reshape(-1)
    select = (target[:, None] == jnp.arange(rows, dtype=I32)[None, :]) & (
        jnp.repeat(owners, capacity)[:, None] == (list_ids // lists)[None, :]
    )
    outgoing = dot(select.astype(BF16), passages).astype(BF16).reshape(devices, capacity, width)
    got_rows = lax.all_to_all(outgoing, AXES, 0, 0, tiled=True)
    local = jnp.sum(jnp.where(select, (list_ids % lists - lists)[None, :], 0), axis=1) + lists
    ids = lax.all_to_all(local.reshape(devices, capacity), AXES, 0, 0, tiled=True).reshape(-1)
    high, low = split_rotation(rotation)
    chunk = 256 if slots % 256 == 0 else slots
    result, centroids = call(
        functools.partial(refine, chunk),
        (got_rows.reshape(slots, width), ids[None, :], ids[:, None], old_centroids, high, low),
        [((slots, width), BF16), ((lists, width), F32)],
        scratch=[((3, lists, width), BF16)],
        limit=48,
    )
    returned = lax.all_to_all(result.reshape(devices, capacity, width), AXES, 0, 0, tiled=True)
    rotated = lax.dot_general(
        select.astype(BF16), returned.reshape(slots, width), (((0,), (0,)), ((), ())), preferred_element_type=F32
    )
    return rotated.astype(BF16), centroids


def shards(passages, list_ids, old_centroids, rotation):
    devices = lax.axis_size("passage") * lax.axis_size("list")
    rows, width = passages.shape
    lists = old_centroids.shape[0]
    capacity = 2 * rows // devices
    if not by_halves(devices, capacity):
        return whole_exchange(passages, list_ids, old_centroids, rotation, devices, capacity)
    half = devices // 2
    pairs = half // 2
    far = half * capacity
    pair = ((2 * capacity, width), BF16)
    unit = 2 * width * width
    me = lax.axis_index(AXES).astype(I32)
    base = jnp.bitwise_and(me, half)
    ids = list_ids[None, :]
    groups = [list(range(half)), list(range(half, devices))]
    rings = [[(i, i ^ (half + 2 * k)) for i in range(devices)] for k in range(pairs)]
    chip = [(i, i ^ 1) for i in range(devices)]

    def shift(a, ring):
        return lax.ppermute(a, AXES, ring)

    def swap_near(a):
        return lax.all_to_all(
            a.reshape(half, capacity, -1), AXES, 0, 0, tiled=True, axis_index_groups=groups
        ).reshape(a.shape)

    def swap_cores(arrived):
        return [shift(a, chip) for a in arrived]

    packed = call(
        functools.partial(pack_far, devices, capacity, lists, pairs // 2),
        (me[None], ids, passages),
        [((1, rows), I32)] + [pair] * pairs,
        limit=62,
        flops=unit * far * rows // width,
    )
    slot = packed[0]
    direct = [shift(a, rings[k]) for k, a in enumerate(packed[1:])]
    local = call(functools.partial(pack_ids, devices, capacity, lists), (ids,), [((devices, capacity), I32)])[0]
    near = call(pack_near, (slot, passages), [((far, width), BF16)], flops=unit * far * rows // width)[0]
    near_rows = swap_near(near)
    got = lax.all_to_all(local, AXES, 0, 0, tiled=True)
    far_ids = jnp.take(got, jnp.bitwise_xor(jnp.arange(half, dtype=I32) + half, me), axis=0, mode="clip")
    near_ids = lax.dynamic_slice_in_dim(got, base, half, 0)
    ids_of_slots = jnp.concatenate([far_ids, near_ids]).reshape(-1)
    col_ids = ids_of_slots[:, None]
    row_ids = ids_of_slots[None, :]
    high, low = split_rotation(rotation)
    slot_col = slot.reshape(rows, 1)
    swapped = swap_cores(direct)

    first = 2
    parts_kind = ((3, lists, width), BF16)
    results = call(
        functools.partial(centre, pairs, first, capacity),
        (*direct, *swapped, near_rows, row_ids, col_ids, old_centroids, high, low),
        [((lists, width), F32), parts_kind, ((far, width), BF16)] + [pair] * first,
        limit=CENTRE,
        flops=unit * 600,
    )
    centroids, parts, held = results[:3]
    back = [shift(a, rings[k]) for k, a in enumerate(results[3:])]
    more = call(
        functools.partial(turn_far, 2 * first * capacity),
        (held, col_ids, parts, high, low),
        [pair] * (pairs - first),
        flops=unit * 1000,
    )
    back += [shift(a, rings[first + k]) for k, a in enumerate(more)]
    result = call(
        functools.partial(turn_near, 2),
        (near_rows, col_ids, parts, high, low),
        [((far, width), BF16)],
        flops=unit * 1500,
    )[0]
    near_back = swap_near(result)
    swapped = swap_cores(back)
    rotated = call(
        functools.partial(unpack, pairs, capacity),
        (*back, *swapped, near_back, slot_col),
        [((rows, width), BF16)],
        scratch=[((far, width), BF16)],
        flops=unit * 512,
    )[0]
    return rotated, centroids


def by_halves(devices, capacity):
    return capacity % TILE == 0 and devices % 16 == 0 and devices & (devices - 1) == 0


def solution(mesh):
    in_specs = (P(AXES, None), P(AXES), P(AXES, None), P())
    out_specs = (P(AXES, None), P(AXES, None))
    return jax.shard_map(shards, mesh=mesh, in_specs=in_specs, out_specs=out_specs, check_vma=False)
```
